128 devices in a mesh: grp: 4 (over z_hi, core), ang: 32 (over x, y, z_lo).
Axes of the slice: x: 4, y: 4, z: 4 (z_hi: 2, z_lo: 2; z = z_hi * 2 + z_lo), core: 2. Of those that a mesh axis runs over, the one named last changes fastest.
Arguments:
- current: bfloat16 [2, 16384, 256], P(None, ('grp', 'ang')), may hold values from -6 to 6
- near_blocks: bfloat16 [5120, 2, 256, 256], P(('grp', 'ang')), may hold values from -0.25 to 0.25
- near_rows: int32 [5120], P(('grp', 'ang')), may hold values from 0 to 127
- near_cols: int32 [5120], P(('grp', 'ang')), may hold values from 0 to 4095
- radiate: float32 [2, 1024, 256], replicated, may hold values from -0.25 to 0.25
- receive: float32 [2, 1024, 256], replicated, may hold values from -0.109375 to 0.109375
- interp: float32 [1536, 1024], replicated, may hold values from -0.1875 to 0.1875
- shift_phase: float32 [8, 1536], replicated, may hold values from -3.140625 to 3.140625
- translate: float32 [2, 316, 1536], P(None, None, 'ang'), may hold values from -0.375 to 0.375
- far_sources: int32 [2048, 16], P('grp'), may hold values from 0 to 2047
- far_types: int32 [2048, 16], P('grp'), may hold values from 0 to 315
Outputs:
- product: float32 [2, 16384, 256], P(None, ('grp', 'ang'))
The draws below stay inside these ranges and needn't reach their ends.
Inputs may be any that keep to these rules, and one draw needn't show every extreme that they name: Block b is stored on device b div 40; near_rows[b] is one of that device's own 128 clusters. near_cols[b] is one of the 4096 clusters of block b's grp index, counted from that group's first cluster. `far_sources`: parent p holds leaf clusters 8 p to 8 p + 7; entries are global parent numbers. `far_types`: an index into the second dimension of translate.
All inputs are finite; a program needn't handle non-finite values.
Results may differ from the reference program's by a relative error of at most 0.0003.
Values may be sent and summed in bfloat16 or wider, within the bound.
A program may use at most 128 MiB of HBM per device.

```python
import math
import jax
import jax.numpy as jnp
import numpy as np
from jax import lax

UNK = 256
K_LEAF = 1024
K_UP = 1536
NT = 316
M_LIST = 16
CL_DEV = 128
NB_DEV = 40
CLUST = 16384
PTOT = 2048
NBLK = 5120
N_GRP = 4
N_ANG = 32


def touch_ends(entries, stream_key, smallest, high):
    shape = entries.shape
    index_at = [jax.random.randint(jax.random.fold_in(stream_key, axis), (), 0, shape[axis]) for axis in range(len(shape))]
    entries = entries.at[tuple(index_at)].set(smallest)
    longest = shape.index(max(shape))
    index_at[longest] = (index_at[longest] + 1) % shape[longest]
    return entries.at[tuple(index_at)].set(high)


def level_of(stream_key, extent, shards, low, largest):
    def one(axis_at, blocks):
        heights = jax.random.uniform(jax.random.fold_in(jax.random.fold_in(stream_key, 6), axis_at), (blocks,), jnp.float32, low / len(shards), largest / len(shards))
        return jnp.repeat(jnp.exp(heights), extent[axis_at] // blocks).reshape((-1,) + (1,) * (len(extent) - axis_at - 1))

    loudness = one(*shards[0])
    for cut in shards[1:]:
        loudness = loudness * one(*cut)
    return loudness


def rank_table(amount, lean):
    weights = [(1 << 20) // math.isqrt(standing ** lean) + 1 for standing in range(1, amount + 1)]
    scale = 1 + sum(weights) // (1 << 30)
    return np.cumsum(np.array([max(1, weight // scale) for weight in weights]))


def ranked_ids(key, shape, count, skew):
    table = rank_table(count, skew)
    lot = jax.random.randint(jax.random.fold_in(key, 1), shape, 0, int(table[count - 1]))
    rank = jnp.searchsorted(jnp.asarray(table, jnp.int32), lot, side="right")
    return jax.random.permutation(jax.random.fold_in(key, 2), count)[rank].astype(jnp.int32)


def gaussian(own_key, shape, scale, bound, cuts=(), held_as=jnp.bfloat16):
    array = jax.random.normal(own_key, shape, jnp.float32) * scale
    if len(cuts) > 0:
        array = level_of(own_key, shape, cuts, -0.22, 0.18) * array
    return jnp.clip(array, min=-bound, max=bound).astype(held_as)


def setup_inputs(seed: int = 0) -> dict:
    seeds = jax.random.split(jax.random.key(seed), 12)
    current = gaussian(seeds[0], (2, CLUST, UNK), 1.0, 6.0, ((1, 128),))
    near_blocks = gaussian(seeds[1], (NBLK, 2, UNK, UNK), (2 * UNK) ** -0.5, 0.25, ((0, 128),))
    near_rows = touch_ends(ranked_ids(seeds[2], (NBLK,), CL_DEV, 2), jax.random.fold_in(seeds[2], 3), 0, CL_DEV - 1).astype(jnp.int32)
    near_cols = touch_ends(jax.random.randint(seeds[3], (NBLK,), 0, CL_DEV * N_ANG), jax.random.fold_in(seeds[3], 1), 0, (CL_DEV * N_ANG) - 1).astype(jnp.int32)
    radiate = gaussian(seeds[4], (2, K_LEAF, UNK), (2 * UNK) ** -0.5, 0.25, (), jnp.float32)
    receive = gaussian(seeds[5], (2, K_LEAF, UNK), (3 * K_LEAF) ** -0.5, 0.109375, (), jnp.float32)
    interp = gaussian(seeds[6], (K_UP, K_LEAF), K_LEAF ** -0.5, 0.1875, (), jnp.float32)
    shift_phase = jnp.clip(jax.random.uniform(seeds[7], (8, K_UP), jnp.float32, -3.140625, 3.140625), -3.140625, 3.140625)
    translate = gaussian(seeds[8], (2, NT, K_UP), (16 * M_LIST) ** -0.5, 0.375, ((2, 32),), jnp.float32)
    far_sources = touch_ends(jax.random.randint(seeds[9], (PTOT, M_LIST), 0, PTOT), jax.random.fold_in(seeds[9], 1), 0, PTOT - 1).astype(jnp.int32)
    far_types = touch_ends(jax.random.randint(seeds[10], (PTOT, M_LIST), 0, NT), jax.random.fold_in(seeds[10], 1), 0, NT - 1).astype(jnp.int32)
    return dict(current=current, near_blocks=near_blocks, near_rows=near_rows, near_cols=near_cols, radiate=radiate, receive=receive, interp=interp, shift_phase=shift_phase, translate=translate, far_sources=far_sources, far_types=far_types)


HIGHEST = lax.Precision.HIGHEST


def complex_product(formula, left_side, right_side):
    real_part = jnp.einsum(formula, left_side[0], right_side[0], precision=HIGHEST) - jnp.einsum(formula, left_side[1], right_side[1], precision=HIGHEST)
    imag_part = jnp.einsum(formula, left_side[0], right_side[1], precision=HIGHEST) + jnp.einsum(formula, left_side[1], right_side[0], precision=HIGHEST)
    return jnp.stack([real_part, imag_part])


def shift_sum(children, cosine, sine_part):
    grouped = children.reshape(2, children.shape[1], children.shape[2] // 8, 8)
    cos_t = cosine.T[:, None, :]
    sin_t = sine_part.T[:, None, :]
    real_part = jnp.sum(cos_t * grouped[0] - sin_t * grouped[1], axis=2)
    imag_part = jnp.sum(cos_t * grouped[1] + sin_t * grouped[0], axis=2)
    return jnp.stack([real_part, imag_part])


def spread(parents, cosine, sine_part):
    cos_t = cosine.T[:, None, :]
    sin_t = sine_part.T[:, None, :]
    par_real = parents[0][:, :, None]
    par_imag = parents[1][:, :, None]
    real_part = cos_t * par_real + sin_t * par_imag
    imag_part = cos_t * par_imag - sin_t * par_real
    width = parents.shape[2] * 8
    return jnp.stack([real_part.reshape(parents.shape[1], width), imag_part.reshape(parents.shape[1], width)])


def reference(current, near_blocks, near_rows, near_cols, radiate, receive, interp, shift_phase, translate, far_sources, far_types):
    as_float = current.astype(jnp.float32)
    cosine = jnp.cos(shift_phase)
    sine_part = jnp.sin(shift_phase)
    radiated = complex_product("kn,cn->kc", radiate, as_float)
    children = jnp.einsum("jk,skc->sjc", interp, radiated, precision=HIGHEST)
    parents = shift_sum(children, cosine, sine_part)

    def add_entry(slot_index, total):
        chosen = jnp.take(parents, far_sources[:, slot_index], axis=2)
        factor = jnp.transpose(jnp.take(translate, far_types[:, slot_index], axis=1), (0, 2, 1))
        real_part = factor[0] * chosen[0] - factor[1] * chosen[1]
        imag_part = factor[0] * chosen[1] + factor[1] * chosen[0]
        return total + jnp.stack([real_part, imag_part])

    incoming = lax.fori_loop(0, M_LIST, add_entry, jnp.zeros(parents.shape, jnp.float32))
    child_in = spread(incoming, cosine, sine_part)
    leaf_in = jnp.einsum("jk,sjc->skc", interp, child_in, precision=HIGHEST)
    far_part = complex_product("kn,kc->cn", receive, leaf_in)

    device_count = N_GRP * N_ANG
    block_ids = jnp.arange(NB_DEV * device_count, dtype=jnp.int32)
    owners = block_ids // NB_DEV
    rows_global = (owners * CL_DEV + near_rows).astype(jnp.int32)
    cols_global = ((owners // N_ANG) * (CL_DEV * N_ANG) + near_cols).astype(jnp.int32)

    def per_device(device_index):
        first_block = (device_index * NB_DEV).astype(jnp.int32)
        block_group = lax.dynamic_slice_in_dim(near_blocks, first_block, NB_DEV, 0).astype(jnp.float32)
        col_ids = lax.dynamic_slice_in_dim(cols_global, first_block, NB_DEV, 0)
        picked = jnp.take(as_float, col_ids, axis=1)
        real_part = jnp.einsum("bmn,bn->bm", block_group[:, 0], picked[0]) - jnp.einsum("bmn,bn->bm", block_group[:, 1], picked[1])
        imag_part = jnp.einsum("bmn,bn->bm", block_group[:, 0], picked[1]) + jnp.einsum("bmn,bn->bm", block_group[:, 1], picked[0])
        return jnp.stack([real_part, imag_part], axis=1)

    contrib = lax.map(per_device, jnp.arange(device_count, dtype=jnp.int32))
    contrib = contrib.reshape(NB_DEV * device_count, 2, UNK)
    near_part = jax.ops.segment_sum(contrib, rows_global, num_segments=CL_DEV * device_count)
    near_part = jnp.transpose(near_part, (1, 0, 2))
    return far_part + near_part
```

```python
import functools

import jax
import jax.numpy as jnp
from jax import lax
from jax.experimental import pallas as pl
from jax.experimental.pallas import tpu as pltpu
from jax.sharding import PartitionSpec as P

HIGH = lax.Precision.HIGH
F32 = jnp.float32
BF16 = jnp.bfloat16


def split_bf16(x):
    hi = lax.reduce_precision(x, exponent_bits=8, mantissa_bits=7)
    lo = (x - hi).astype(BF16)
    return hi.astype(BF16), lo


def near_kernel(blocks_per_step, rows_ref, cols_ref, cur_ref, blk_ref, out_ref):
    step = pl.program_id(0)

    @pl.when(step == 0)
    def _():
        out_ref[...] = jnp.zeros_like(out_ref)

    unk = blk_ref.shape[-1]
    for k in range(blocks_per_step):
        b = step * blocks_per_step + k
        col = cols_ref[b]
        row = rows_ref[b]
        base = pl.multiple_of((col // 16) * 16, 16)
        tile = cur_ref[pl.ds(base, 16), :].astype(F32)
        pick = lax.broadcasted_iota(jnp.int32, tile.shape, 0) == (col % 16)
        x = jnp.sum(jnp.where(pick, tile, 0.0), axis=0, keepdims=True).astype(BF16)
        xs = jnp.concatenate([x[:, :unk], x[:, unk:]], axis=0)
        dims = (((1,), (1,)), ((), ()))
        r = lax.dot_general(xs, blk_ref[k, 0], dims, preferred_element_type=F32)
        i = lax.dot_general(xs, blk_ref[k, 1], dims, preferred_element_type=F32)
        re = r[0:1] - i[1:2]
        im = r[1:2] + i[0:1]
        out_ref[pl.ds(row, 1), pl.ds(0, unk)] += re
        out_ref[pl.ds(row, 1), pl.ds(unk, unk)] += im


def near_product(gathered, near_blocks, near_rows, near_cols, own_count):
    nblk, _, unk, _ = near_blocks.shape
    per_step = 8
    grid_spec = pltpu.PrefetchScalarGridSpec(
        num_scalar_prefetch=2,
        grid=(nblk // per_step,),
        in_specs=[
            pl.BlockSpec(gathered.shape, lambda i, r, c: (0, 0)),
            pl.BlockSpec((per_step, 2, unk, unk), lambda i, r, c: (i, 0, 0, 0)),
        ],
        out_specs=pl.BlockSpec((own_count, 2 * unk), lambda i, r, c: (0, 0)),
    )
    return pl.pallas_call(
        functools.partial(near_kernel, per_step),
        grid_spec=grid_spec,
        out_shape=jax.ShapeDtypeStruct((own_count, 2 * unk), F32),
        compiler_params=pltpu.CompilerParams(
            dimension_semantics=("arbitrary",), vmem_limit_bytes=48 * 1024 * 1024
        ),
        cost_estimate=pl.CostEstimate(
            flops=8 * nblk * unk * unk,
            bytes_accessed=near_blocks.size * 2 + gathered.size * 2,
            transcendentals=0,
        ),
    )(near_rows, near_cols, gathered, near_blocks)


def on_device(
    current,
    near_blocks,
    near_rows,
    near_cols,
    radiate,
    receive,
    interp,
    shift_phase,
    translate,
    far_sources,
    far_types,
):
    _, own_count, unk = current.shape
    k_leaf = radiate.shape[1]
    k_up = interp.shape[0]

    cur_flat = jnp.transpose(current, (1, 0, 2)).reshape(own_count, 2 * unk)
    gathered = lax.all_gather(cur_flat, "ang", axis=0, tiled=True)
    near_flat = near_product(gathered, near_blocks, near_rows, near_cols, own_count)
    near_part = jnp.transpose(near_flat.reshape(own_count, 2, unk), (1, 0, 2))

    cosine = jnp.cos(shift_phase)
    sine_part = jnp.sin(shift_phase)

    rr_hi, rr_lo = split_bf16(radiate[0])
    ri_hi, ri_lo = split_bf16(radiate[1])
    lhs = jnp.concatenate([rr_hi, rr_lo, ri_hi, ri_lo], axis=0)
    rhs = jnp.concatenate([current[0], current[1]], axis=0)
    prod = jnp.einsum("kn,cn->kc", lhs, rhs, preferred_element_type=F32)
    prod = prod.reshape(4, k_leaf, 2, own_count)
    rr = prod[0] + prod[1]
    ri = prod[2] + prod[3]
    rad_re = rr[:, 0] - ri[:, 1]
    rad_im = rr[:, 1] + ri[:, 0]
    radiated = jnp.concatenate([rad_re, rad_im], axis=1)

    children = jnp.dot(interp, radiated, precision=HIGH, preferred_element_type=F32)
    grouped = children.reshape(k_up, 2, own_count // 8, 8)
    cos_t = cosine.T[:, None, :]
    sin_t = sine_part.T[:, None, :]
    par_re = jnp.sum(cos_t * grouped[:, 0] - sin_t * grouped[:, 1], axis=2)
    par_im = jnp.sum(cos_t * grouped[:, 1] + sin_t * grouped[:, 0], axis=2)
    own_parents = jnp.stack([par_re, par_im])

    parents = lax.all_to_all(own_parents, "ang", split_axis=1, concat_axis=2, tiled=True)
    n_s, j_loc, p_grp = parents.shape
    sources = lax.all_gather(parents.reshape(1, n_s * j_loc, p_grp), "grp", axis=0, tiled=True)
    n_grp = sources.shape[0]
    s_hi, s_lo = split_bf16(sources)
    s_split = jnp.concatenate([s_hi, s_lo], axis=1)

    t_local = translate.reshape(2, translate.shape[1], j_loc)
    t2 = jnp.transpose(t_local, (0, 2, 1)).reshape(2 * j_loc, translate.shape[1])
    t_hi, t_lo = split_bf16(t2)
    t_split = jnp.concatenate([t_hi, t_lo], axis=0)

    parent_ids = jnp.arange(n_grp * p_grp, dtype=jnp.int32).reshape(n_grp, p_grp)
    kind_ids = jnp.arange(translate.shape[1], dtype=jnp.int32)
    rows = 2 * j_loc
    inc_re = jnp.zeros((j_loc, p_grp), F32)
    inc_im = jnp.zeros((j_loc, p_grp), F32)
    for m in range(far_sources.shape[1]):
        src = far_sources[:, m]
        typ = far_types[:, m]
        onehot_src = (parent_ids[:, :, None] == src[None, None, :]).astype(BF16)
        chosen2 = jnp.einsum("gaq,gqp->ap", s_split, onehot_src, preferred_element_type=F32)
        chosen = chosen2[:rows] + chosen2[rows:]
        onehot_kind = (kind_ids[:, None] == typ[None, :]).astype(BF16)
        factor2 = jnp.dot(t_split, onehot_kind, preferred_element_type=F32)
        factor = factor2[:rows] + factor2[rows:]
        c_re, c_im = chosen[:j_loc], chosen[j_loc:]
        f_re, f_im = factor[:j_loc], factor[j_loc:]
        inc_re = inc_re + (f_re * c_re - f_im * c_im)
        inc_im = inc_im + (f_re * c_im + f_im * c_re)
    incoming = jnp.stack([inc_re, inc_im])

    returned = lax.all_to_all(incoming, "ang", split_axis=2, concat_axis=1, tiled=True)
    r_re = returned[0][:, :, None]
    r_im = returned[1][:, :, None]
    ci_re = (cos_t * r_re + sin_t * r_im).reshape(k_up, own_count)
    ci_im = (cos_t * r_im - sin_t * r_re).reshape(k_up, own_count)
    child_in = jnp.concatenate([ci_re, ci_im], axis=1)
    leaf_in = jnp.einsum("jk,jx->kx", interp, child_in, precision=HIGH, preferred_element_type=F32)

    recv = jnp.concatenate([receive[0], receive[1]], axis=1)
    far = jnp.einsum("kx,kn->xn", leaf_in, recv, precision=HIGH, preferred_element_type=F32)
    far = far.reshape(2, own_count, 2, unk)
    far_re = far[0, :, 0] - far[1, :, 1]
    far_im = far[1, :, 0] + far[0, :, 1]
    far_part = jnp.stack([far_re, far_im])
    return far_part + near_part


def solution(mesh):
    in_specs = (
        P(None, ("grp", "ang"), None),
        P(("grp", "ang"), None, None, None),
        P(("grp", "ang")),
        P(("grp", "ang")),
        P(),
        P(),
        P(),
        P(),
        P(None, None, "ang"),
        P("grp", None),
        P("grp", None),
    )
    out_specs = P(None, ("grp", "ang"), None)
    return jax.shard_map(
        on_device, mesh=mesh, in_specs=in_specs, out_specs=out_specs, check_vma=False
    )
```

```python
import functools

import jax
import jax.numpy as jnp
from jax import lax
from jax.experimental import pallas as pl
from jax.experimental.pallas import tpu as pltpu
from jax.sharding import PartitionSpec as P

HIGH = lax.Precision.HIGH
F32 = jnp.float32
BF16 = jnp.bfloat16


def split_bf16(x):
    hi = lax.reduce_precision(x, exponent_bits=8, mantissa_bits=7)
    lo = (x - hi).astype(BF16)
    return hi.astype(BF16), lo


def near_kernel(blocks_per_step, rows_ref, cols_ref, cur_ref, blk_ref, out_ref):
    step = pl.program_id(0)

    @pl.when(step == 0)
    def _():
        out_ref[...] = jnp.zeros_like(out_ref)

    unk = blk_ref.shape[-1]
    for k in range(blocks_per_step):
        b = step * blocks_per_step + k
        col = cols_ref[b]
        row = rows_ref[b]
        base = pl.multiple_of((col // 16) * 16, 16)
        tile = cur_ref[pl.ds(base, 16), :].astype(F32)
        pick = lax.broadcasted_iota(jnp.int32, tile.shape, 0) == (col % 16)
        x = jnp.sum(jnp.where(pick, tile, 0.0), axis=0, keepdims=True).astype(BF16)
        xs = jnp.concatenate([x[:, :unk], x[:, unk:]], axis=0)
        dims = (((1,), (1,)), ((), ()))
        r = lax.dot_general(xs, blk_ref[k, 0], dims, preferred_element_type=F32)
        i = lax.dot_general(xs, blk_ref[k, 1], dims, preferred_element_type=F32)
        re = r[0:1] - i[1:2]
        im = r[1:2] + i[0:1]
        out_ref[pl.ds(row, 1), pl.ds(0, unk)] += re
        out_ref[pl.ds(row, 1), pl.ds(unk, unk)] += im


def near_product(gathered, near_blocks, near_rows, near_cols, own_count):
    nblk, _, unk, _ = near_blocks.shape
    per_step = 8
    grid_spec = pltpu.PrefetchScalarGridSpec(
        num_scalar_prefetch=2,
        grid=(nblk // per_step,),
        in_specs=[
            pl.BlockSpec(gathered.shape, lambda i, r, c: (0, 0)),
            pl.BlockSpec((per_step, 2, unk, unk), lambda i, r, c: (i, 0, 0, 0)),
        ],
        out_specs=pl.BlockSpec((own_count, 2 * unk), lambda i, r, c: (0, 0)),
    )
    return pl.pallas_call(
        functools.partial(near_kernel, per_step),
        grid_spec=grid_spec,
        out_shape=jax.ShapeDtypeStruct((own_count, 2 * unk), F32),
        compiler_params=pltpu.CompilerParams(
            dimension_semantics=("arbitrary",), vmem_limit_bytes=48 * 1024 * 1024
        ),
        cost_estimate=pl.CostEstimate(
            flops=8 * nblk * unk * unk,
            bytes_accessed=near_blocks.size * 2 + gathered.size * 2,
            transcendentals=0,
        ),
    )(near_rows, near_cols, gathered, near_blocks)


def on_device(
    current,
    near_blocks,
    near_rows,
    near_cols,
    radiate,
    receive,
    interp,
    shift_phase,
    translate,
    far_sources,
    far_types,
):
    _, own_count, unk = current.shape
    k_leaf = radiate.shape[1]
    k_up = interp.shape[0]

    cur_flat = jnp.transpose(current, (1, 0, 2)).reshape(own_count, 2 * unk)
    n_ang = lax.axis_size("ang")
    spread_copies = jnp.broadcast_to(cur_flat[None], (n_ang,) + cur_flat.shape)
    gathered = lax.all_to_all(spread_copies, "ang", split_axis=0, concat_axis=0, tiled=True)
    gathered = gathered.reshape(n_ang * own_count, 2 * unk)
    near_flat = near_product(gathered, near_blocks, near_rows, near_cols, own_count)
    near_part = jnp.transpose(near_flat.reshape(own_count, 2, unk), (1, 0, 2))

    cosine = jnp.cos(shift_phase)
    sine_part = jnp.sin(shift_phase)

    rr_hi, rr_lo = split_bf16(radiate[0])
    ri_hi, ri_lo = split_bf16(radiate[1])
    lhs = jnp.concatenate([rr_hi, rr_lo, ri_hi, ri_lo], axis=0)
    rhs = jnp.concatenate([current[0], current[1]], axis=0)
    prod = jnp.einsum("kn,cn->kc", lhs, rhs, preferred_element_type=F32)
    prod = prod.reshape(4, k_leaf, 2, own_count)
    rr = prod[0] + prod[1]
    ri = prod[2] + prod[3]
    rad_re = rr[:, 0] - ri[:, 1]
    rad_im = rr[:, 1] + ri[:, 0]
    radiated = jnp.concatenate([rad_re, rad_im], axis=1)

    children = jnp.dot(interp, radiated, precision=HIGH, preferred_element_type=F32)
    grouped = children.reshape(k_up, 2, own_count // 8, 8)
    cos_t = cosine.T[:, None, :]
    sin_t = sine_part.T[:, None, :]
    par_re = jnp.sum(cos_t * grouped[:, 0] - sin_t * grouped[:, 1], axis=2)
    par_im = jnp.sum(cos_t * grouped[:, 1] + sin_t * grouped[:, 0], axis=2)
    own_parents = jnp.stack([par_re, par_im])

    parents = lax.all_to_all(own_parents, "ang", split_axis=1, concat_axis=2, tiled=True)
    n_s, j_loc, p_grp = parents.shape
    sources = lax.all_gather(parents.reshape(1, n_s * j_loc, p_grp), "grp", axis=0, tiled=True)
    n_grp = sources.shape[0]
    s_hi, s_lo = split_bf16(sources)
    s_split = jnp.concatenate([s_hi, s_lo], axis=1)

    t_local = translate.reshape(2, translate.shape[1], j_loc)
    t2 = jnp.transpose(t_local, (0, 2, 1)).reshape(2 * j_loc, translate.shape[1])
    t_hi, t_lo = split_bf16(t2)
    t_split = jnp.concatenate([t_hi, t_lo], axis=0)

    parent_ids = jnp.arange(n_grp * p_grp, dtype=jnp.int32).reshape(n_grp, p_grp)
    kind_ids = jnp.arange(translate.shape[1], dtype=jnp.int32)
    rows = 2 * j_loc
    inc_re = jnp.zeros((j_loc, p_grp), F32)
    inc_im = jnp.zeros((j_loc, p_grp), F32)
    for m in range(far_sources.shape[1]):
        src = far_sources[:, m]
        typ = far_types[:, m]
        onehot_src = (parent_ids[:, :, None] == src[None, None, :]).astype(BF16)
        chosen2 = jnp.einsum("gaq,gqp->ap", s_split, onehot_src, preferred_element_type=F32)
        chosen = chosen2[:rows] + chosen2[rows:]
        onehot_kind = (kind_ids[:, None] == typ[None, :]).astype(BF16)
        factor2 = jnp.dot(t_split, onehot_kind, preferred_element_type=F32)
        factor = factor2[:rows] + factor2[rows:]
        c_re, c_im = chosen[:j_loc], chosen[j_loc:]
        f_re, f_im = factor[:j_loc], factor[j_loc:]
        inc_re = inc_re + (f_re * c_re - f_im * c_im)
        inc_im = inc_im + (f_re * c_im + f_im * c_re)
    incoming = jnp.stack([inc_re, inc_im])

    returned = lax.all_to_all(incoming, "ang", split_axis=2, concat_axis=1, tiled=True)
    r_re = returned[0][:, :, None]
    r_im = returned[1][:, :, None]
    ci_re = (cos_t * r_re + sin_t * r_im).reshape(k_up, own_count)
    ci_im = (cos_t * r_im - sin_t * r_re).reshape(k_up, own_count)
    child_in = jnp.concatenate([ci_re, ci_im], axis=1)
    leaf_in = jnp.einsum("jk,jx->kx", interp, child_in, precision=HIGH, preferred_element_type=F32)

    recv = jnp.concatenate([receive[0], receive[1]], axis=1)
    far = jnp.einsum("kx,kn->xn", leaf_in, recv, precision=HIGH, preferred_element_type=F32)
    far = far.reshape(2, own_count, 2, unk)
    far_re = far[0, :, 0] - far[1, :, 1]
    far_im = far[1, :, 0] + far[0, :, 1]
    far_part = jnp.stack([far_re, far_im])
    return far_part + near_part


def solution(mesh):
    in_specs = (
        P(None, ("grp", "ang"), None),
        P(("grp", "ang"), None, None, None),
        P(("grp", "ang")),
        P(("grp", "ang")),
        P(),
        P(),
        P(),
        P(),
        P(None, None, "ang"),
        P("grp", None),
        P("grp", None),
    )
    out_specs = P(None, ("grp", "ang"), None)
    return jax.shard_map(
        on_device, mesh=mesh, in_specs=in_specs, out_specs=out_specs, check_vma=False
    )
```

```python
import functools

import jax
import jax.numpy as jnp
from jax import lax
from jax.experimental import pallas as pl
from jax.experimental.pallas import tpu as pltpu
from jax.sharding import PartitionSpec as P

HIGH = lax.Precision.HIGH
F32 = jnp.float32
BF16 = jnp.bfloat16


def split_bf16(x):
    hi = lax.reduce_precision(x, exponent_bits=8, mantissa_bits=7)
    lo = (x - hi).astype(BF16)
    return hi.astype(BF16), lo


def near_kernel(blocks_per_step, own_count, nblk, rows_ref, cols_ref, cur_ref, blk_ref, out_ref):
    step = pl.program_id(0)

    @pl.when(step == 0)
    def _():
        out_ref[...] = jnp.zeros_like(out_ref)

    unk = blk_ref.shape[-1]
    for k in range(blocks_per_step):
        b = step * blocks_per_step + k
        col = (cols_ref[b] // own_count) * nblk + b
        row = rows_ref[b]
        base = pl.multiple_of((col // 16) * 16, 16)
        tile = cur_ref[pl.ds(base, 16), :].astype(F32)
        pick = lax.broadcasted_iota(jnp.int32, tile.shape, 0) == (col % 16)
        x = jnp.sum(jnp.where(pick, tile, 0.0), axis=0, keepdims=True).astype(BF16)
        xs = jnp.concatenate([x[:, :unk], x[:, unk:]], axis=0)
        dims = (((1,), (1,)), ((), ()))
        r = lax.dot_general(xs, blk_ref[k, 0], dims, preferred_element_type=F32)
        i = lax.dot_general(xs, blk_ref[k, 1], dims, preferred_element_type=F32)
        re = r[0:1] - i[1:2]
        im = r[1:2] + i[0:1]
        out_ref[pl.ds(row, 1), pl.ds(0, unk)] += re
        out_ref[pl.ds(row, 1), pl.ds(unk, unk)] += im


def near_product(gathered, near_blocks, near_rows, near_cols, own_count):
    nblk, _, unk, _ = near_blocks.shape
    per_step = 8
    grid_spec = pltpu.PrefetchScalarGridSpec(
        num_scalar_prefetch=2,
        grid=(nblk // per_step,),
        in_specs=[
            pl.BlockSpec(gathered.shape, lambda i, r, c: (0, 0)),
            pl.BlockSpec((per_step, 2, unk, unk), lambda i, r, c: (i, 0, 0, 0)),
        ],
        out_specs=pl.BlockSpec((own_count, 2 * unk), lambda i, r, c: (0, 0)),
    )
    return pl.pallas_call(
        functools.partial(near_kernel, per_step, own_count, nblk),
        grid_spec=grid_spec,
        out_shape=jax.ShapeDtypeStruct((own_count, 2 * unk), F32),
        compiler_params=pltpu.CompilerParams(
            dimension_semantics=("arbitrary",), vmem_limit_bytes=48 * 1024 * 1024
        ),
        cost_estimate=pl.CostEstimate(
            flops=8 * nblk * unk * unk,
            bytes_accessed=near_blocks.size * 2 + gathered.size * 2,
            transcendentals=0,
        ),
    )(near_rows, near_cols, gathered, near_blocks)


def on_device(
    current,
    near_blocks,
    near_rows,
    near_cols,
    radiate,
    receive,
    interp,
    shift_phase,
    translate,
    far_sources,
    far_types,
):
    _, own_count, unk = current.shape
    k_leaf = radiate.shape[1]
    k_up = interp.shape[0]

    cur_flat = jnp.transpose(current, (1, 0, 2)).reshape(own_count, 2 * unk)
    n_ang = lax.axis_size("ang")
    my_ang = lax.axis_index("ang")
    cols_all = lax.all_gather(near_cols, "ang", axis=0, tiled=False)
    local_ids = cols_all - my_ang * own_count
    onehot_rows = (
        local_ids[:, :, None] == jnp.arange(own_count, dtype=jnp.int32)[None, None, :]
    ).astype(BF16)
    requested = jnp.einsum(
        "akc,cx->akx", onehot_rows, cur_flat, preferred_element_type=F32
    ).astype(BF16)
    delivered = lax.all_to_all(requested, "ang", split_axis=0, concat_axis=0, tiled=True)
    delivered = delivered.reshape(n_ang * near_cols.shape[0], 2 * unk)
    near_flat = near_product(delivered, near_blocks, near_rows, near_cols, own_count)
    near_part = jnp.transpose(near_flat.reshape(own_count, 2, unk), (1, 0, 2))

    cosine = jnp.cos(shift_phase)
    sine_part = jnp.sin(shift_phase)

    rr_hi, rr_lo = split_bf16(radiate[0])
    ri_hi, ri_lo = split_bf16(radiate[1])
    lhs = jnp.concatenate([rr_hi, rr_lo, ri_hi, ri_lo], axis=0)
    rhs = jnp.concatenate([current[0], current[1]], axis=0)
    prod = jnp.einsum("kn,cn->kc", lhs, rhs, preferred_element_type=F32)
    prod = prod.reshape(4, k_leaf, 2, own_count)
    rr = prod[0] + prod[1]
    ri = prod[2] + prod[3]
    rad_re = rr[:, 0] - ri[:, 1]
    rad_im = rr[:, 1] + ri[:, 0]
    radiated = jnp.concatenate([rad_re, rad_im], axis=1)

    children = jnp.dot(interp, radiated, precision=HIGH, preferred_element_type=F32)
    grouped = children.reshape(k_up, 2, own_count // 8, 8)
    cos_t = cosine.T[:, None, :]
    sin_t = sine_part.T[:, None, :]
    par_re = jnp.sum(cos_t * grouped[:, 0] - sin_t * grouped[:, 1], axis=2)
    par_im = jnp.sum(cos_t * grouped[:, 1] + sin_t * grouped[:, 0], axis=2)
    own_parents = jnp.stack([par_re, par_im])

    parents = lax.all_to_all(own_parents, "ang", split_axis=1, concat_axis=2, tiled=True)
    n_s, j_loc, p_grp = parents.shape
    sources = lax.all_gather(parents.reshape(1, n_s * j_loc, p_grp), "grp", axis=0, tiled=True)
    n_grp = sources.shape[0]
    s_hi, s_lo = split_bf16(sources)
    s_split = jnp.concatenate([s_hi, s_lo], axis=1)

    t_local = translate.reshape(2, translate.shape[1], j_loc)
    t2 = jnp.transpose(t_local, (0, 2, 1)).reshape(2 * j_loc, translate.shape[1])
    t_hi, t_lo = split_bf16(t2)
    t_split = jnp.concatenate([t_hi, t_lo], axis=0)

    parent_ids = jnp.arange(n_grp * p_grp, dtype=jnp.int32).reshape(n_grp, p_grp)
    kind_ids = jnp.arange(translate.shape[1], dtype=jnp.int32)
    rows = 2 * j_loc
    inc_re = jnp.zeros((j_loc, p_grp), F32)
    inc_im = jnp.zeros((j_loc, p_grp), F32)
    for m in range(far_sources.shape[1]):
        src = far_sources[:, m]
        typ = far_types[:, m]
        onehot_src = (parent_ids[:, :, None] == src[None, None, :]).astype(BF16)
        chosen2 = jnp.einsum("gaq,gqp->ap", s_split, onehot_src, preferred_element_type=F32)
        chosen = chosen2[:rows] + chosen2[rows:]
        onehot_kind = (kind_ids[:, None] == typ[None, :]).astype(BF16)
        factor2 = jnp.dot(t_split, onehot_kind, preferred_element_type=F32)
        factor = factor2[:rows] + factor2[rows:]
        c_re, c_im = chosen[:j_loc], chosen[j_loc:]
        f_re, f_im = factor[:j_loc], factor[j_loc:]
        inc_re = inc_re + (f_re * c_re - f_im * c_im)
        inc_im = inc_im + (f_re * c_im + f_im * c_re)
    incoming = jnp.stack([inc_re, inc_im])

    returned = lax.all_to_all(incoming, "ang", split_axis=2, concat_axis=1, tiled=True)
    r_re = returned[0][:, :, None]
    r_im = returned[1][:, :, None]
    ci_re = (cos_t * r_re + sin_t * r_im).reshape(k_up, own_count)
    ci_im = (cos_t * r_im - sin_t * r_re).reshape(k_up, own_count)
    child_in = jnp.concatenate([ci_re, ci_im], axis=1)
    leaf_in = jnp.einsum("jk,jx->kx", interp, child_in, precision=HIGH, preferred_element_type=F32)

    recv = jnp.concatenate([receive[0], receive[1]], axis=1)
    far = jnp.einsum("kx,kn->xn", leaf_in, recv, precision=HIGH, preferred_element_type=F32)
    far = far.reshape(2, own_count, 2, unk)
    far_re = far[0, :, 0] - far[1, :, 1]
    far_im = far[1, :, 0] + far[0, :, 1]
    far_part = jnp.stack([far_re, far_im])
    return far_part + near_part


def solution(mesh):
    in_specs = (
        P(None, ("grp", "ang"), None),
        P(("grp", "ang"), None, None, None),
        P(("grp", "ang")),
        P(("grp", "ang")),
        P(),
        P(),
        P(),
        P(),
        P(None, None, "ang"),
        P("grp", None),
        P("grp", None),
    )
    out_specs = P(None, ("grp", "ang"), None)
    return jax.shard_map(
        on_device, mesh=mesh, in_specs=in_specs, out_specs=out_specs, check_vma=False
    )
```
